32 devices in a mesh: cell: 2 (over core), gene: 4 (over y, x), rank: 4 (over z).
Axes of the slice: x: 2, y: 2, z: 4, core: 2. Of those that a mesh axis runs over, the one named last changes fastest.
Arguments:
- blocks: bfloat16 [2, 16, 96, 256, 128], P('cell', ('gene', 'rank')), may hold values from -6 to 6
- block_pos: int32 [2, 16, 96], P('cell', ('gene', 'rank')), may hold values from 0 to 127, as said below
- block_count: int32 [2, 16], P('cell', ('gene', 'rank')), may hold values from 32 to 96, as said below
- test_right: bfloat16 [32768, 512], P(('gene', 'rank')), may hold values from -0.0625 to 0.0625
- test_left: bfloat16 [4096, 768], P('cell', 'rank'), may hold values from -0.1875 to 0.1875
- gene_sketch_old: float32 [768, 32768], P('cell', ('gene', 'rank')), may hold values from -4 to 4
Outputs:
- right_sketch: float32 [4096, 512], P(('cell', 'gene', 'rank'))
- gene_sketch: float32 [768, 32768], P('cell', ('gene', 'rank'))
- core: float32 [768, 512], P('cell')
The draws below stay inside these ranges and needn't reach their ends.
Inputs may be any that keep to these rules, and one draw needn't show every extreme that they name: `block_pos`: position p names row block p // 16 and gene block p % 16 of the device's tile; the 96 positions of one device are distinct. `block_count`: some device has all 96 slots live in every draw; slots from the count on are not part of A.
All inputs are finite; a program needn't handle non-finite values.
Results may differ from the reference program's by a relative error of at most 0.0003.
Values may be sent and summed in bfloat16 or wider, within the bound.
A program may use at most 128 MiB of HBM per device.

```python
import jax
import jax.numpy as jnp
from jax import lax

BROWS = 256
BCOLS = 128
R = 512
L = 768
GB_DEV = 16
RB_DEV = 8
NB = 96
CSHARDS = 2
GSHARDS = 16
CELLS = 4096
GENES = 32768
N_CELL = 2
N_GENE = 4
N_RANK = 4


def draw_block_pos(key, part):
    devices = CSHARDS * GSHARDS
    tile_size = RB_DEV * GB_DEV
    subkeys = jax.random.split(key, devices)
    orders = jax.vmap(lambda single: jax.random.permutation(single, tile_size))(subkeys)
    return orders[:, :NB].reshape(CSHARDS, GSHARDS, NB).astype(jnp.int32)


def draw_block_count(key, part):
    first_key, second_key = jax.random.split(jax.random.fold_in(key, 7))
    devices = CSHARDS * GSHARDS
    spread = jax.random.randint(first_key, (devices,), 0, 65)
    floor_count = NB // 3
    counts = floor_count + (NB - floor_count) * spread * spread // 4096
    chosen = jax.random.randint(second_key, (), 0, devices)
    counts = jnp.where(jnp.arange(devices) == chosen, NB, counts)
    return counts.reshape(CSHARDS, GSHARDS).astype(jnp.int32)


def block_scale(stream_key, extent, cuts, least, high):
    gain = 1.0
    for dim, shards_of in cuts:
        heights = jax.random.uniform(jax.random.fold_in(jax.random.fold_in(stream_key, 6), dim), (shards_of,), jnp.float32, least / len(cuts), high / len(cuts))
        gain = gain * jnp.repeat(jnp.exp(heights), extent[dim] // shards_of).reshape((-1,) + (1,) * (len(extent) - 1 - dim))
    return gain


def scatter_about(stream_key, extent, deviation, bound, pieces=(), kind=jnp.bfloat16):
    loudness = block_scale(stream_key, extent, pieces, -0.22, 0.18) if pieces else 1.0
    values = jax.random.normal(stream_key, extent, jnp.float32) * deviation * loudness
    return jnp.minimum(jnp.maximum(values, -bound), bound).astype(kind)


def setup_inputs(seed: int = 0) -> dict:
    key_list = jax.random.split(jax.random.key(seed), 7)
    return {
        "blocks": scatter_about(key_list[0], (N_CELL, N_GENE * N_RANK, NB, BROWS, BCOLS), 1.0, 6.0, ((0, 2), (1, 16))),
        "block_pos": draw_block_pos(jax.random.fold_in(key_list[6], 71), 0),
        "block_count": draw_block_count(jax.random.fold_in(key_list[6], 71), 0),
        "test_right": scatter_about(key_list[3], (GENES, R), (GENES // 4) ** -0.5, 0.0625, ((0, 16),)),
        "test_left": scatter_about(key_list[4], (CELLS, L), (CELLS // 4) ** -0.5, 0.1875, ((0, 2), (1, 4))),
        "gene_sketch_old": scatter_about(key_list[5], (L, GENES), 0.5, 4.0, ((0, 2), (1, 16)), jnp.float32),
    }


def reference(blocks, block_pos, block_count, test_right, test_left, gene_sketch_old):
    highest = lax.Precision.HIGHEST
    cell_rows = RB_DEV * BROWS
    gene_cols = GB_DEV * BCOLS
    right_table = test_right.reshape(GSHARDS * GB_DEV, BCOLS, R)
    left_table = test_left.reshape(CSHARDS * RB_DEV, BROWS, L)
    slot_ids = jnp.arange(NB, dtype=jnp.int32)
    row_ids = jnp.arange(RB_DEV, dtype=jnp.int32)
    gene_ids = jnp.arange(GB_DEV, dtype=jnp.int32)

    def visit(carry, flat_index):
        right_acc, gene_acc = carry
        cell_index = flat_index // GSHARDS
        gene_index = flat_index % GSHARDS
        tiles = blocks[cell_index, gene_index].astype(jnp.float32)
        positions = block_pos[cell_index, gene_index]
        alive_mask = (slot_ids < block_count[cell_index, gene_index]).astype(jnp.float32)
        row_block = positions // GB_DEV
        gene_block = positions % GB_DEV
        right_rows = right_table[gene_index * GB_DEV + gene_block].astype(jnp.float32)
        left_rows = left_table[cell_index * RB_DEV + row_block].astype(jnp.float32)
        right_terms = jnp.einsum("pik,pkr->pir", tiles, right_rows, precision=highest) * alive_mask[:, None, None]
        gene_terms = jnp.einsum("pil,pik->plk", left_rows, tiles, precision=highest) * alive_mask[:, None, None]
        row_hot = (row_block[None, :] == row_ids[:, None]).astype(jnp.float32)
        gene_hot = (gene_block[None, :] == gene_ids[:, None]).astype(jnp.float32)
        right_tile = jnp.einsum("rp,pik->rik", row_hot, right_terms, precision=highest).reshape(cell_rows, R)
        gene_tile = jnp.einsum("gp,plk->lgk", gene_hot, gene_terms, precision=highest).reshape(L, gene_cols)
        row_start = (cell_index * cell_rows).astype(jnp.int32)
        col_start = (gene_index * gene_cols).astype(jnp.int32)
        anchor = jnp.zeros((), jnp.int32)
        old_rows = lax.dynamic_slice(right_acc, (row_start, anchor), (cell_rows, R))
        right_acc = lax.dynamic_update_slice(right_acc, old_rows + right_tile, (row_start, anchor))
        old_cols = lax.dynamic_slice(gene_acc, (anchor, col_start), (L, gene_cols))
        gene_acc = lax.dynamic_update_slice(gene_acc, old_cols + gene_tile, (anchor, col_start))
        return (right_acc, gene_acc), None

    initial = (jnp.zeros((CSHARDS * cell_rows, R), jnp.float32), jnp.zeros((L, GSHARDS * gene_cols), jnp.float32))
    (right_sketch, gene_sum), unused = lax.scan(visit, initial, jnp.arange(CSHARDS * GSHARDS, dtype=jnp.int32))
    core = lax.dot_general(test_left.astype(jnp.float32), right_sketch, (((0,), (0,)), ((), ())), precision=highest)
    return right_sketch, gene_sketch_old + gene_sum, core
```

```python
import functools

import jax
import jax.numpy as jnp
from jax import lax
from jax.experimental import pallas as pl
from jax.experimental.pallas import tpu as pltpu
from jax.sharding import PartitionSpec as P

MESH = pl.DeviceIdType.MESH
GENE_CHUNK = 256


def kernel(
    sizes, code, blocks, right_in, left_in, right_out, gene_out, core_out,
    tiles, dense, table, left, part, hop1, hop2, hopz,
    core_part, core_cell, core_gene, core_rank, gene_send, gene_recv,
    load_sem, agz_s, agz_r, agx_s, agx_r, rs1_s, rs1_r, rs2_s, rs2_r, rsz_s, rsz_r,
    cc_s, cc_r, cg_s, cg_r, cr_s, cr_r, ar_s, ar_r, ag_s, ag_r, gs_s, gs_r,
):
    n_cell, n_gene, n_rank = sizes
    f32, bf16 = jnp.float32, jnp.bfloat16
    c, g, r = lax.axis_index("cell"), lax.axis_index("gene"), lax.axis_index("rank")
    b1, b0 = g // 2, g % 2
    gx = 2 * b1 + (1 - b0)
    gy = 2 * (1 - b1) + b0
    gd = 2 * (1 - b1) + (1 - b0)
    gene_peers = [gx, gy, gd]
    rows, width = part.shape
    quarter = rows // n_gene
    shard = quarter // n_rank
    half = width // 2
    lw = left_in.shape[0]
    left_width = left.shape[0]
    brows, bcols = tiles.shape[1], tiles.shape[2]
    gene_blocks = dense.shape[1] // bcols
    share = left_width // n_cell
    core_rows = share // n_gene
    lanes = width // n_rank

    def rank_of(k):
        return lax.rem(r + k, n_rank)

    def cell_of(k):
        return lax.rem(c + k, n_cell)

    def cut(start, step):
        return pl.ds(pl.multiple_of(start * step, step), step)

    def remote(src, dst, ssem, rsem, **where):
        device = (where.get("cell", c), where.get("gene", g), where.get("rank", r))
        return pltpu.make_async_remote_copy(
            src_ref=src, dst_ref=dst, send_sem=ssem, recv_sem=rsem,
            device_id=device, device_id_type=MESH,
        )

    barrier = pltpu.get_barrier_semaphore()
    for k in range(1, n_rank):
        pl.semaphore_signal(barrier, inc=1, device_id=(c, g, rank_of(k)), device_id_type=MESH)
    for peer in gene_peers:
        pl.semaphore_signal(barrier, inc=1, device_id=(c, peer, r), device_id_type=MESH)
    for k in range(1, n_cell):
        pl.semaphore_signal(barrier, inc=1, device_id=(cell_of(k), g, r), device_id_type=MESH)

    load_tiles = pltpu.make_async_copy(blocks, tiles, load_sem.at[0])
    load_table = pltpu.make_async_copy(right_in, table, load_sem.at[1])
    load_tiles.start()
    load_table.start()
    own_left = []
    for i, q in enumerate((g, gd)):
        copy = pltpu.make_async_copy(
            left_in.at[:, cut(q, quarter)], left.at[cut(r, lw), cut(q, quarter)], load_sem.at[2 + i]
        )
        copy.start()
        own_left.append(copy)

    pl.semaphore_wait(barrier, (n_rank - 1) + len(gene_peers) + (n_cell - 1))

    agz = []
    for i, q in enumerate((g, gd)):
        for k in range(1, n_rank):
            s = i * (n_rank - 1) + k - 1
            copy = remote(
                left_in.at[:, cut(q, quarter)], left.at[cut(r, lw), cut(q, quarter)],
                agz_s.at[s], agz_r.at[s], rank=rank_of(k),
            )
            copy.start()
            agz.append(copy)
    load_tiles.wait()
    load_table.wait()

    row_blocks = quarter // brows

    def compute(q):
        def fill(i, carry):
            rb = q * row_blocks + i // gene_blocks
            gb = i % gene_blocks
            slot = code[rb * gene_blocks + gb]
            block = tiles[jnp.maximum(slot - 1, 0)]
            dense[cut(rb, brows), cut(gb, bcols)] = jnp.where(slot > 0, block, jnp.zeros_like(block))
            return carry

        lax.fori_loop(0, row_blocks * gene_blocks, fill, 0)

        def multiply(h, carry):
            part[cut(q, quarter), cut(h, half)] = jnp.dot(
                dense[cut(q, quarter), :], table[:, cut(h, half)], preferred_element_type=f32
            )
            return carry

        lax.fori_loop(0, 2, multiply, 0)

    h0, h1 = pl.ds(0, half), pl.ds(half, half)

    def rs1(i, q, h, peer):
        copy = remote(part.at[cut(q, quarter), h], hop1.at[i], rs1_s.at[i], rs1_r.at[i], gene=peer)
        copy.start()
        return copy

    compute(gd)
    d0 = rs1(0, gd, h0, gx)
    d1 = rs1(1, gd, h1, gy)
    compute(gx)
    o0 = rs1(2, gx, h0, gx)
    compute(gy)
    o1 = rs1(3, gy, h1, gy)
    compute(g)

    order = [rank_of(k) for k in range(1, n_rank)] + [r]
    second = []
    for i, (first, q, h, peer) in enumerate(((d0, gy, h0, gy), (d1, gx, h1, gx))):
        first.wait_recv()
        copies = []
        for j, z in enumerate(order):
            here = pl.ds(pl.multiple_of(q * quarter + z * shard, shard), shard)
            part[here, h] = part[here, h] + hop1[i, cut(z, shard), :]
            copy = remote(
                part.at[here, h], hop2.at[i, cut(z, shard), :],
                rs2_s.at[i * n_rank + j], rs2_r.at[i * n_rank + j], gene=peer,
            )
            copy.start()
            copies.append(copy)
        second.append(copies)

    for copy in own_left:
        copy.wait()
    for copy in agz[: n_rank - 1]:
        copy.wait_recv()
    agx = []
    for i, peer in enumerate((gx, gy)):
        copy = remote(
            left.at[:, cut(g, quarter)], left.at[:, cut(g, quarter)], agx_s.at[i], agx_r.at[i], gene=peer
        )
        copy.start()
        agx.append(copy)

    o0.wait_recv()
    o1.wait_recv()
    rsz = []
    for j, z in enumerate(order):
        second[0][j].wait_recv()
        second[1][j].wait_recv()
        here = pl.ds(pl.multiple_of(g * quarter + z * shard, shard), shard)
        part[here, h0] = part[here, h0] + hop1[2, cut(z, shard), :] + hop2[0, cut(z, shard), :]
        part[here, h1] = part[here, h1] + hop1[3, cut(z, shard), :] + hop2[1, cut(z, shard), :]
        if j < n_rank - 1:
            copy = remote(part.at[here, :], hopz.at[j], rsz_s.at[j], rsz_r.at[j], rank=z)
            copy.start()
            rsz.append(copy)
    for copy in rsz:
        copy.wait_recv()
    mine_at = pl.ds(pl.multiple_of(g * quarter + r * shard, shard), shard)
    mine = part[mine_at, :]
    for j in range(n_rank - 1):
        mine = mine + hopz[j]
    right_out[...] = mine

    hi = mine.astype(bf16)
    rest = mine - hi.astype(f32)
    mid = rest.astype(bf16)
    low = (rest - mid.astype(f32)).astype(bf16)
    left_mine = left[:, mine_at]
    core_part[...] = (
        jnp.dot(left_mine, hi, preferred_element_type=f32)
        + jnp.dot(left_mine, mid, preferred_element_type=f32)
        + jnp.dot(left_mine, low, preferred_element_type=f32)
    )
    own_share = cut(c, share)
    cc = []
    for k in range(1, n_cell):
        copy = remote(
            core_part.at[cut(cell_of(k), share), :], core_cell.at[k - 1],
            cc_s.at[k - 1], cc_r.at[k - 1], cell=cell_of(k),
        )
        copy.start()
        cc.append(copy)
    for k in range(1, n_cell):
        cc[k - 1].wait_recv()
        core_part[own_share, :] = core_part[own_share, :] + core_cell[k - 1]
    cg = []
    for i, peer in enumerate(gene_peers):
        src = pl.ds(pl.multiple_of(c * share + peer * core_rows, 8), core_rows)
        copy = remote(core_part.at[src, :], core_gene.at[i], cg_s.at[i], cg_r.at[i], gene=peer)
        copy.start()
        cg.append(copy)

    for copy in agz[n_rank - 1 :]:
        copy.wait_recv()
    for copy in agx:
        copy.wait_recv()
    chunks = dense.shape[1] // GENE_CHUNK

    def gene_copy(k, j):
        return remote(
            gene_send.at[k - 1, :, cut(j, GENE_CHUNK)], gene_recv.at[k - 1, :, cut(j, GENE_CHUNK)],
            gs_s.at[k - 1, j], gs_r.at[k - 1, j], cell=cell_of(k),
        )

    for k in range(1, n_cell):
        peer_rows = cut(cell_of(k), share)

        def send_chunk(j, carry):
            gene_send[k - 1, :, cut(j, GENE_CHUNK)] = jnp.dot(
                left[peer_rows, :], dense[:, cut(j, GENE_CHUNK)], preferred_element_type=f32
            )
            gene_copy(k, j).start()
            return carry

        lax.fori_loop(0, chunks, send_chunk, 0)

    own_rows = pl.ds(pl.multiple_of(c * share + g * core_rows, 8), core_rows)
    for i in range(len(gene_peers)):
        cg[i].wait_recv()
        core_part[own_rows, :] = core_part[own_rows, :] + core_gene[i]
    cr = []
    for k in range(1, n_rank):
        copy = remote(
            core_part.at[own_rows, cut(rank_of(k), lanes)], core_rank.at[k - 1],
            cr_s.at[k - 1], cr_r.at[k - 1], rank=rank_of(k),
        )
        copy.start()
        cr.append(copy)

    def own_chunk(j, carry):
        gene_out[:, cut(j, GENE_CHUNK)] = jnp.dot(
            left[own_share, :], dense[:, cut(j, GENE_CHUNK)], preferred_element_type=f32
        )
        return carry

    lax.fori_loop(0, chunks // 2, own_chunk, 0)

    final = core_part[own_rows, cut(r, lanes)]
    for k in range(1, n_rank):
        cr[k - 1].wait_recv()
        final = final + core_rank[k - 1]
    out_rows = pl.ds(pl.multiple_of(g * core_rows, 8), core_rows)
    core_out[out_rows, cut(r, lanes)] = final
    ar = []
    for k in range(1, n_rank):
        copy = remote(
            core_out.at[out_rows, cut(r, lanes)], core_out.at[out_rows, cut(r, lanes)],
            ar_s.at[k - 1], ar_r.at[k - 1], rank=rank_of(k),
        )
        copy.start()
        ar.append(copy)

    lax.fori_loop(chunks // 2, chunks, own_chunk, 0)

    for copy in ar:
        copy.wait_recv()
    ag = []
    for i, peer in enumerate(gene_peers):
        copy = remote(core_out.at[out_rows, :], core_out.at[out_rows, :], ag_s.at[i], ag_r.at[i], gene=peer)
        copy.start()
        ag.append(copy)

    for k in range(1, n_cell):

        def add_chunk(j, carry):
            gene_copy(k, j).wait_recv()
            here = cut(j, GENE_CHUNK)
            gene_out[:, here] = gene_out[:, here] + gene_recv[k - 1, :, here]
            return carry

        lax.fori_loop(0, chunks, add_chunk, 0)

    for copy in ag:
        copy.wait_recv()

    for copy in agz + agx + [d0, d1, o0, o1] + second[0] + second[1] + rsz + cc + cg + cr + ar + ag:
        copy.wait_send()
    for k in range(1, n_cell):

        def drain(j, carry):
            gene_copy(k, j).wait_send()
            return carry

        lax.fori_loop(0, chunks, drain, 0)


def body(sizes, blocks, block_pos, block_count, test_right, test_left, gene_sketch_old):
    n_cell, n_gene, n_rank = sizes
    f32, bf16 = jnp.float32, jnp.bfloat16
    tiles = blocks[0, 0]
    slots, brows, bcols = tiles.shape
    genes, width = test_right.shape
    rows, lw = test_left.shape
    left_width = lw * n_rank
    gene_blocks = genes // bcols
    places = (rows // brows) * gene_blocks
    slot_ids = jnp.arange(slots, dtype=jnp.int32)
    hit = (block_pos[0, 0][None, :] == jnp.arange(places, dtype=jnp.int32)[:, None]) & (
        slot_ids < block_count[0, 0]
    )[None, :]
    code = jnp.sum(jnp.where(hit, slot_ids[None, :] + 1, 0), axis=1).astype(jnp.int32)
    quarter, half = rows // n_gene, width // 2
    shard = quarter // n_rank
    share = left_width // n_cell
    core_rows, lanes = share // n_gene, width // n_rank
    chunks = genes // GENE_CHUNK
    dma = pltpu.SemaphoreType.DMA
    z, x = n_rank - 1, n_gene - 1

    def pair(*shape):
        return [dma(shape), dma(shape)]

    right_mine, gene_sum, core = pl.pallas_call(
        functools.partial(kernel, sizes),
        out_shape=(
            jax.ShapeDtypeStruct((shard, width), f32),
            jax.ShapeDtypeStruct((share, genes), f32),
            jax.ShapeDtypeStruct((share, width), f32),
        ),
        in_specs=[
            pl.BlockSpec(memory_space=pltpu.SMEM),
            pl.BlockSpec(memory_space=pl.ANY),
            pl.BlockSpec(memory_space=pl.ANY),
            pl.BlockSpec(memory_space=pl.ANY),
        ],
        out_specs=tuple(pl.BlockSpec(memory_space=pltpu.VMEM) for _ in range(3)),
        scratch_shapes=[
            pltpu.VMEM((slots, brows, bcols), bf16),
            pltpu.VMEM((rows, genes), bf16),
            pltpu.VMEM((genes, width), bf16),
            pltpu.VMEM((left_width, rows), bf16),
            pltpu.VMEM((rows, width), f32),
            pltpu.VMEM((4, quarter, half), f32),
            pltpu.VMEM((2, quarter, half), f32),
            pltpu.VMEM((z, shard, width), f32),
            pltpu.VMEM((left_width, width), f32),
            pltpu.VMEM((n_cell - 1, share, width), f32),
            pltpu.VMEM((x, core_rows, width), f32),
            pltpu.VMEM((z, core_rows, lanes), f32),
            pltpu.VMEM((n_cell - 1, share, genes), f32),
            pltpu.VMEM((n_cell - 1, share, genes), f32),
            dma((4,)),
            *pair(2 * z),
            *pair(2),
            *pair(4),
            *pair(2 * n_rank),
            *pair(z),
            *pair(n_cell - 1),
            *pair(x),
            *pair(z),
            *pair(z),
            *pair(x),
            *pair(n_cell - 1, chunks),
        ],
        compiler_params=pltpu.CompilerParams(
            collective_id=0, has_side_effects=True, vmem_limit_bytes=62 * 1024 * 1024
        ),
        name="sketch",
    )(code, tiles, test_right, test_left.T)
    return right_mine, gene_sketch_old + gene_sum, core


def solution(mesh):
    sizes = tuple(mesh.shape[name] for name in ("cell", "gene", "rank"))
    return jax.shard_map(
        functools.partial(body, sizes),
        mesh=mesh,
        in_specs=(
            P("cell", ("gene", "rank"), None, None, None),
            P("cell", ("gene", "rank"), None),
            P("cell", ("gene", "rank")),
            P(("gene", "rank"), None),
            P("cell", "rank"),
            P("cell", ("gene", "rank")),
        ),
        out_specs=(P(("cell", "gene", "rank"), None), P("cell", ("gene", "rank")), P("cell", None)),
        check_vma=False,
    )
```

```python
import functools

import jax
import jax.numpy as jnp
from jax import lax
from jax.experimental import pallas as pl
from jax.experimental.pallas import tpu as pltpu
from jax.sharding import PartitionSpec as P

MESH = pl.DeviceIdType.MESH
GENE_CHUNK = 256


def kernel(
    sizes, code, blocks, right_in, left_in, right_out, gene_out, core_out,
    tiles, dense, table, left, part, hop1, hop2, hopz,
    core_part, core_cell, core_gene, core_rank, gene_send, gene_recv,
    load_sem, agz_s, agz_r, agx_s, agx_r, rs1_s, rs1_r, rs2_s, rs2_r, rsz_s, rsz_r,
    cc_s, cc_r, cg_s, cg_r, cr_s, cr_r, ar_s, ar_r, ag_s, ag_r, gs_s, gs_r,
):
    n_cell, n_gene, n_rank = sizes
    f32, bf16 = jnp.float32, jnp.bfloat16
    c, g, r = lax.axis_index("cell"), lax.axis_index("gene"), lax.axis_index("rank")
    b1, b0 = g // 2, g % 2
    gx = 2 * b1 + (1 - b0)
    gy = 2 * (1 - b1) + b0
    gd = 2 * (1 - b1) + (1 - b0)
    gene_peers = [gx, gy, gd]
    rows, width = part.shape
    quarter = rows // n_gene
    shard = quarter // n_rank
    half = width // 2
    lw = left_in.shape[0]
    left_width = left.shape[0]
    brows, bcols = tiles.shape[1], tiles.shape[2]
    gene_blocks = dense.shape[1] // bcols
    share = left_width // n_cell
    core_rows = share // n_gene
    lanes = width // n_rank

    def rank_of(k):
        return lax.rem(r + k, n_rank)

    def cell_of(k):
        return lax.rem(c + k, n_cell)

    def cut(start, step):
        return pl.ds(pl.multiple_of(start * step, step), step)

    def remote(src, dst, ssem, rsem, **where):
        device = (where.get("cell", c), where.get("gene", g), where.get("rank", r))
        return pltpu.make_async_remote_copy(
            src_ref=src, dst_ref=dst, send_sem=ssem, recv_sem=rsem,
            device_id=device, device_id_type=MESH,
        )

    barrier = pltpu.get_barrier_semaphore()
    for k in range(1, n_rank):
        pl.semaphore_signal(barrier, inc=1, device_id=(c, g, rank_of(k)), device_id_type=MESH)
    for peer in gene_peers:
        pl.semaphore_signal(barrier, inc=1, device_id=(c, peer, r), device_id_type=MESH)
    for k in range(1, n_cell):
        pl.semaphore_signal(barrier, inc=1, device_id=(cell_of(k), g, r), device_id_type=MESH)

    load_tiles = pltpu.make_async_copy(blocks, tiles, load_sem.at[0])
    load_table = pltpu.make_async_copy(right_in, table, load_sem.at[1])
    load_tiles.start()
    load_table.start()
    own_left = []
    for i, q in enumerate((g, gd)):
        copy = pltpu.make_async_copy(
            left_in.at[:, cut(q, quarter)], left.at[cut(r, lw), cut(q, quarter)], load_sem.at[2 + i]
        )
        copy.start()
        own_left.append(copy)

    pl.semaphore_wait(barrier, (n_rank - 1) + len(gene_peers) + (n_cell - 1))

    agz = []
    for i, q in enumerate((g, gd)):
        for k in range(1, n_rank):
            s = i * (n_rank - 1) + k - 1
            copy = remote(
                left_in.at[:, cut(q, quarter)], left.at[cut(r, lw), cut(q, quarter)],
                agz_s.at[s], agz_r.at[s], rank=rank_of(k),
            )
            copy.start()
            agz.append(copy)
    load_tiles.wait()
    load_table.wait()

    row_blocks = quarter // brows

    def compute(q):
        def fill(i, carry):
            rb = q * row_blocks + i // gene_blocks
            gb = i % gene_blocks
            slot = code[rb * gene_blocks + gb]
            block = tiles[jnp.maximum(slot - 1, 0)]
            dense[cut(rb, brows), cut(gb, bcols)] = jnp.where(slot > 0, block, jnp.zeros_like(block))
            return carry

        lax.fori_loop(0, row_blocks * gene_blocks, fill, 0)

        def multiply(h, carry):
            part[cut(q, quarter), cut(h, half)] = jnp.dot(
                dense[cut(q, quarter), :], table[:, cut(h, half)], preferred_element_type=f32
            )
            return carry

        lax.fori_loop(0, 2, multiply, 0)

    h0, h1 = pl.ds(0, half), pl.ds(half, half)

    def rs1(i, q, h, peer):
        copy = remote(part.at[cut(q, quarter), h], hop1.at[i], rs1_s.at[i], rs1_r.at[i], gene=peer)
        copy.start()
        return copy

    compute(gd)
    d0 = rs1(0, gd, h0, gx)
    d1 = rs1(1, gd, h1, gy)
    compute(gx)
    o0 = rs1(2, gx, h0, gx)
    compute(gy)
    o1 = rs1(3, gy, h1, gy)
    compute(g)

    order = [rank_of(k) for k in range(1, n_rank)] + [r]
    second = []
    for i, (first, q, h, peer) in enumerate(((d0, gy, h0, gy), (d1, gx, h1, gx))):
        first.wait_recv()
        copies = []
        for j, z in enumerate(order):
            here = pl.ds(pl.multiple_of(q * quarter + z * shard, shard), shard)
            part[here, h] = part[here, h] + hop1[i, cut(z, shard), :]
            copy = remote(
                part.at[here, h], hop2.at[i, cut(z, shard), :],
                rs2_s.at[i * n_rank + j], rs2_r.at[i * n_rank + j], gene=peer,
            )
            copy.start()
            copies.append(copy)
        second.append(copies)

    for copy in own_left:
        copy.wait()
    for copy in agz[: n_rank - 1]:
        copy.wait_recv()
    agx = []

    def send_left(k):
        for i, peer in enumerate((gx, gy)):
            here = left.at[cut(cell_of(k), share), cut(g, quarter)]
            copy = remote(here, here, agx_s.at[k, i], agx_r.at[k, i], gene=peer)
            copy.start()
            agx.append(copy)

    for k in range(1, n_cell):
        send_left(k)

    o0.wait_recv()
    o1.wait_recv()
    rsz = []
    for j, z in enumerate(order):
        second[0][j].wait_recv()
        second[1][j].wait_recv()
        here = pl.ds(pl.multiple_of(g * quarter + z * shard, shard), shard)
        part[here, h0] = part[here, h0] + hop1[2, cut(z, shard), :] + hop2[0, cut(z, shard), :]
        part[here, h1] = part[here, h1] + hop1[3, cut(z, shard), :] + hop2[1, cut(z, shard), :]
        if j < n_rank - 1:
            copy = remote(part.at[here, :], hopz.at[j], rsz_s.at[j], rsz_r.at[j], rank=z)
            copy.start()
            rsz.append(copy)
    def core_rows_of(k):
        at = cut(cell_of(k), share)

        def multiply(h, carry):
            here = cut(h, half)
            mine = part[cut(g, quarter), here]
            hi = mine.astype(bf16)
            rest = mine - hi.astype(f32)
            mid = rest.astype(bf16)
            low = (rest - mid.astype(f32)).astype(bf16)
            rows_left = left[at, cut(g, quarter)]
            core_part[at, here] = (
                jnp.dot(rows_left, hi, preferred_element_type=f32)
                + jnp.dot(rows_left, mid, preferred_element_type=f32)
                + jnp.dot(rows_left, low, preferred_element_type=f32)
            )
            return carry

        lax.fori_loop(0, 2, multiply, 0)

    own_share = cut(c, share)
    cc = []
    for k in range(1, n_cell):
        core_rows_of(k)
        copy = remote(
            core_part.at[cut(cell_of(k), share), :], core_cell.at[k - 1],
            cc_s.at[k - 1], cc_r.at[k - 1], cell=cell_of(k),
        )
        copy.start()
        cc.append(copy)
    core_rows_of(0)
    for k in range(1, n_cell):
        cc[k - 1].wait_recv()
        core_part[own_share, :] = core_part[own_share, :] + core_cell[k - 1]
    cg = []
    for i, peer in enumerate(gene_peers):
        src = pl.ds(pl.multiple_of(c * share + peer * core_rows, 8), core_rows)
        copy = remote(core_part.at[src, :], core_gene.at[i], cg_s.at[i], cg_r.at[i], gene=peer)
        copy.start()
        cg.append(copy)
    send_left(0)

    for copy in agz[n_rank - 1 :]:
        copy.wait_recv()
    for copy in agx[:-2]:
        copy.wait_recv()
    chunks = dense.shape[1] // GENE_CHUNK

    def gene_copy(k, j):
        return remote(
            gene_send.at[k - 1, :, cut(j, GENE_CHUNK)], gene_recv.at[k - 1, :, cut(j, GENE_CHUNK)],
            gs_s.at[k - 1, j], gs_r.at[k - 1, j], cell=cell_of(k),
        )

    for k in range(1, n_cell):
        peer_rows = cut(cell_of(k), share)

        def send_chunk(j, carry):
            gene_send[k - 1, :, cut(j, GENE_CHUNK)] = jnp.dot(
                left[peer_rows, :], dense[:, cut(j, GENE_CHUNK)], preferred_element_type=f32
            )
            gene_copy(k, j).start()
            return carry

        lax.fori_loop(0, chunks, send_chunk, 0)

    own_rows = pl.ds(pl.multiple_of(c * share + g * core_rows, 8), core_rows)
    for i in range(len(gene_peers)):
        cg[i].wait_recv()
        core_part[own_rows, :] = core_part[own_rows, :] + core_gene[i]
    cr = []
    for k in range(1, n_rank):
        copy = remote(
            core_part.at[own_rows, cut(rank_of(k), lanes)], core_rank.at[k - 1],
            cr_s.at[k - 1], cr_r.at[k - 1], rank=rank_of(k),
        )
        copy.start()
        cr.append(copy)

    final = core_part[own_rows, cut(r, lanes)]
    for k in range(1, n_rank):
        cr[k - 1].wait_recv()
        final = final + core_rank[k - 1]
    out_rows = pl.ds(pl.multiple_of(g * core_rows, 8), core_rows)
    core_out[out_rows, cut(r, lanes)] = final
    own_piece = core_out.at[out_rows, cut(r, lanes)]
    ar = []
    for k in range(1, n_rank):
        copy = remote(own_piece, own_piece, ar_s.at[k - 1], ar_r.at[k - 1], rank=rank_of(k))
        copy.start()
        ar.append(copy)
    ag = []

    def spread(k):
        piece = core_out.at[out_rows, cut(rank_of(n_rank - k), lanes)]
        for i, peer in enumerate(gene_peers):
            copy = remote(piece, piece, ag_s.at[k, i], ag_r.at[k, i], gene=peer)
            copy.start()
            ag.append(copy)

    spread(0)
    for k in range(1, n_rank):
        ar[k - 1].wait_recv()
        spread(k)

    for copy in agx[-2:]:
        copy.wait_recv()

    def own_chunk(j, carry):
        here = cut(j, GENE_CHUNK)
        gene_out[:, here] = jnp.dot(left[own_share, :], dense[:, here], preferred_element_type=f32)
        return carry

    lax.fori_loop(0, chunks, own_chunk, 0)

    for k in range(1, n_cell):

        def add_chunk(j, carry):
            gene_copy(k, j).wait_recv()
            here = cut(j, GENE_CHUNK)
            gene_out[:, here] = gene_out[:, here] + gene_recv[k - 1, :, here]
            return carry

        lax.fori_loop(0, chunks, add_chunk, 0)

    for copy in rsz:
        copy.wait_recv()
    mine = part[pl.ds(pl.multiple_of(g * quarter + r * shard, shard), shard), :]
    for j in range(n_rank - 1):
        mine = mine + hopz[j]
    right_out[...] = mine
    for copy in ag:
        copy.wait_recv()

    for copy in agz + agx + [d0, d1, o0, o1] + second[0] + second[1] + rsz + cc + cg + cr + ar + ag:
        copy.wait_send()
    for k in range(1, n_cell):

        def drain(j, carry):
            gene_copy(k, j).wait_send()
            return carry

        lax.fori_loop(0, chunks, drain, 0)


def body(sizes, blocks, block_pos, block_count, test_right, test_left, gene_sketch_old):
    n_cell, n_gene, n_rank = sizes
    f32, bf16 = jnp.float32, jnp.bfloat16
    tiles = blocks[0, 0]
    slots, brows, bcols = tiles.shape
    genes, width = test_right.shape
    rows, lw = test_left.shape
    left_width = lw * n_rank
    gene_blocks = genes // bcols
    places = (rows // brows) * gene_blocks
    slot_ids = jnp.arange(slots, dtype=jnp.int32)
    hit = (block_pos[0, 0][None, :] == jnp.arange(places, dtype=jnp.int32)[:, None]) & (
        slot_ids < block_count[0, 0]
    )[None, :]
    code = jnp.sum(jnp.where(hit, slot_ids[None, :] + 1, 0), axis=1).astype(jnp.int32)
    quarter, half = rows // n_gene, width // 2
    shard = quarter // n_rank
    share = left_width // n_cell
    core_rows, lanes = share // n_gene, width // n_rank
    chunks = genes // GENE_CHUNK
    dma = pltpu.SemaphoreType.DMA
    z, x = n_rank - 1, n_gene - 1

    def pair(*shape):
        return [dma(shape), dma(shape)]

    right_mine, gene_sum, core = pl.pallas_call(
        functools.partial(kernel, sizes),
        out_shape=(
            jax.ShapeDtypeStruct((shard, width), f32),
            jax.ShapeDtypeStruct((share, genes), f32),
            jax.ShapeDtypeStruct((share, width), f32),
        ),
        in_specs=[
            pl.BlockSpec(memory_space=pltpu.SMEM),
            pl.BlockSpec(memory_space=pltpu.HBM),
            pl.BlockSpec(memory_space=pltpu.HBM),
            pl.BlockSpec(memory_space=pltpu.HBM),
        ],
        out_specs=tuple(pl.BlockSpec(memory_space=pltpu.VMEM) for _ in range(3)),
        scratch_shapes=[
            pltpu.VMEM((slots, brows, bcols), bf16),
            pltpu.VMEM((rows, genes), bf16),
            pltpu.VMEM((genes, width), bf16),
            pltpu.VMEM((left_width, rows), bf16),
            pltpu.VMEM((rows, width), f32),
            pltpu.VMEM((4, quarter, half), f32),
            pltpu.VMEM((2, quarter, half), f32),
            pltpu.VMEM((z, shard, width), f32),
            pltpu.VMEM((left_width, width), f32),
            pltpu.VMEM((n_cell - 1, share, width), f32),
            pltpu.VMEM((x, core_rows, width), f32),
            pltpu.VMEM((z, core_rows, lanes), f32),
            pltpu.VMEM((n_cell - 1, share, genes), f32),
            pltpu.VMEM((n_cell - 1, share, genes), f32),
            dma((4,)),
            *pair(2 * z),
            *pair(n_cell, 2),
            *pair(4),
            *pair(2 * n_rank),
            *pair(z),
            *pair(n_cell - 1),
            *pair(x),
            *pair(z),
            *pair(z),
            *pair(n_rank, x),
            *pair(n_cell - 1, chunks),
        ],
        compiler_params=pltpu.CompilerParams(
            collective_id=0, has_side_effects=True, vmem_limit_bytes=46 * 1024 * 1024
        ),
        name="sketch",
    )(code, tiles, test_right, test_left.T)
    return right_mine, gene_sketch_old + gene_sum, core


def solution(mesh):
    sizes = tuple(mesh.shape[name] for name in ("cell", "gene", "rank"))
    return jax.shard_map(
        functools.partial(body, sizes),
        mesh=mesh,
        in_specs=(
            P("cell", ("gene", "rank"), None, None, None),
            P("cell", ("gene", "rank"), None),
            P("cell", ("gene", "rank")),
            P(("gene", "rank"), None),
            P("cell", "rank"),
            P("cell", ("gene", "rank")),
        ),
        out_specs=(P(("cell", "gene", "rank"), None), P("cell", ("gene", "rank")), P("cell", None)),
        check_vma=False,
    )
```

```python
import functools

import jax
import jax.numpy as jnp
from jax import lax
from jax.experimental import pallas as pl
from jax.experimental.pallas import tpu as pltpu
from jax.sharding import PartitionSpec as P

MESH = pl.DeviceIdType.MESH
GENE_CHUNK = 256


def kernel(
    sizes, code, blocks, right_in, left_in, right_out, gene_out, core_out,
    tiles, dense, table, left, part, hop1, hop2, hopz,
    core_part, core_cell, core_gene, core_rank, gene_send, gene_recv,
    load_sem, agz_s, agz_r, agx_s, agx_r, rs1_s, rs1_r, rs2_s, rs2_r, rsz_s, rsz_r,
    cc_s, cc_r, cg_s, cg_r, cr_s, cr_r, ar_s, ar_r, ag_s, ag_r, gs_s, gs_r,
):
    n_cell, n_gene, n_rank = sizes
    f32, bf16 = jnp.float32, jnp.bfloat16
    c, g, r = lax.axis_index("cell"), lax.axis_index("gene"), lax.axis_index("rank")
    b1, b0 = g // 2, g % 2
    gx = 2 * b1 + (1 - b0)
    gy = 2 * (1 - b1) + b0
    gd = 2 * (1 - b1) + (1 - b0)
    gene_peers = [gx, gy, gd]
    rows, width = part.shape
    quarter = rows // n_gene
    shard = quarter // n_rank
    half = width // 2
    lw = left_in.shape[0]
    left_width = left.shape[0]
    brows, bcols = tiles.shape[1], tiles.shape[2]
    gene_blocks = dense.shape[1] // bcols
    share = left_width // n_cell
    core_rows = share // n_gene
    lanes = width // n_rank

    def rank_of(k):
        return lax.rem(r + k, n_rank)

    def cell_of(k):
        return lax.rem(c + k, n_cell)

    def cut(start, step):
        return pl.ds(pl.multiple_of(start * step, step), step)

    def remote(src, dst, ssem, rsem, **where):
        device = (where.get("cell", c), where.get("gene", g), where.get("rank", r))
        return pltpu.make_async_remote_copy(
            src_ref=src, dst_ref=dst, send_sem=ssem, recv_sem=rsem,
            device_id=device, device_id_type=MESH,
        )

    barrier = pltpu.get_barrier_semaphore()
    for k in range(1, n_rank):
        pl.semaphore_signal(barrier, inc=1, device_id=(c, g, rank_of(k)), device_id_type=MESH)
    for peer in gene_peers:
        pl.semaphore_signal(barrier, inc=1, device_id=(c, peer, r), device_id_type=MESH)
    for k in range(1, n_cell):
        pl.semaphore_signal(barrier, inc=1, device_id=(cell_of(k), g, r), device_id_type=MESH)

    load_tiles = pltpu.make_async_copy(blocks, tiles, load_sem.at[0])
    load_table = pltpu.make_async_copy(right_in, table, load_sem.at[1])
    load_tiles.start()
    load_table.start()
    own_left = []
    for i, q in enumerate((g, gd)):
        copy = pltpu.make_async_copy(
            left_in.at[:, cut(q, quarter)], left.at[cut(r, lw), cut(q, quarter)], load_sem.at[2 + i]
        )
        copy.start()
        own_left.append(copy)

    pl.semaphore_wait(barrier, (n_rank - 1) + len(gene_peers) + (n_cell - 1))

    agz = []
    for i, q in enumerate((g, gd)):
        for k in range(1, n_rank):
            s = i * (n_rank - 1) + k - 1
            copy = remote(
                left_in.at[:, cut(q, quarter)], left.at[cut(r, lw), cut(q, quarter)],
                agz_s.at[s], agz_r.at[s], rank=rank_of(k),
            )
            copy.start()
            agz.append(copy)
    agx = []
    for i, peer in enumerate((gx, gy)):
        copy = remote(
            left_in.at[:, cut(g, quarter)], left.at[cut(r, lw), cut(g, quarter)],
            agx_s.at[n_rank, i], agx_r.at[n_rank, i], gene=peer,
        )
        copy.start()
        agx.append(copy)
    load_tiles.wait()
    load_table.wait()

    row_blocks = quarter // brows

    def compute(q):
        def fill(i, carry):
            rb = q * row_blocks + i // gene_blocks
            gb = i % gene_blocks
            slot = code[rb * gene_blocks + gb]
            block = tiles[jnp.maximum(slot - 1, 0)]
            dense[cut(rb, brows), cut(gb, bcols)] = jnp.where(slot > 0, block, jnp.zeros_like(block))
            return carry

        lax.fori_loop(0, row_blocks * gene_blocks, fill, 0)

        def multiply(h, carry):
            part[cut(q, quarter), cut(h, half)] = jnp.dot(
                dense[cut(q, quarter), :], table[:, cut(h, half)], preferred_element_type=f32
            )
            return carry

        lax.fori_loop(0, 2, multiply, 0)

    h0, h1 = pl.ds(0, half), pl.ds(half, half)

    def rs1(i, q, h, peer):
        copy = remote(part.at[cut(q, quarter), h], hop1.at[i], rs1_s.at[i], rs1_r.at[i], gene=peer)
        copy.start()
        return copy

    compute(gd)
    d0 = rs1(0, gd, h0, gx)
    d1 = rs1(1, gd, h1, gy)
    compute(gx)
    o0 = rs1(2, gx, h0, gx)
    compute(gy)
    o1 = rs1(3, gy, h1, gy)
    compute(g)

    order = [rank_of(k) for k in range(1, n_rank)] + [r]
    second = []
    for i, (first, q, h, peer) in enumerate(((d0, gy, h0, gy), (d1, gx, h1, gx))):
        first.wait_recv()
        copies = []
        for j, z in enumerate(order):
            here = pl.ds(pl.multiple_of(q * quarter + z * shard, shard), shard)
            part[here, h] = part[here, h] + hop1[i, cut(z, shard), :]
            copy = remote(
                part.at[here, h], hop2.at[i, cut(z, shard), :],
                rs2_s.at[i * n_rank + j], rs2_r.at[i * n_rank + j], gene=peer,
            )
            copy.start()
            copies.append(copy)
        second.append(copies)

    for copy in own_left:
        copy.wait()
    for copy in agz[: n_rank - 1]:
        copy.wait_recv()
    per_share = 0 if n_rank % n_cell else n_rank // n_cell
    lead = n_rank - per_share
    base = (c + 1) * per_share

    def left_piece(j, act):
        z = lax.rem(base + j, n_rank)
        here = left.at[cut(z, lw), cut(g, quarter)]

        @pl.when(z != r)
        def _():
            for i, peer in enumerate((gx, gy)):
                act(remote(here, here, agx_s.at[j, i], agx_r.at[j, i], gene=peer))

    for j in range(lead):
        left_piece(j, lambda copy: copy.start())

    o0.wait_recv()
    o1.wait_recv()
    rsz = []
    for j, z in enumerate(order):
        second[0][j].wait_recv()
        second[1][j].wait_recv()
        here = pl.ds(pl.multiple_of(g * quarter + z * shard, shard), shard)
        part[here, h0] = part[here, h0] + hop1[2, cut(z, shard), :] + hop2[0, cut(z, shard), :]
        part[here, h1] = part[here, h1] + hop1[3, cut(z, shard), :] + hop2[1, cut(z, shard), :]
        if j < n_rank - 1:
            copy = remote(part.at[here, :], hopz.at[j], rsz_s.at[j], rsz_r.at[j], rank=z)
            if j < n_rank - 2:
                copy.start()
            rsz.append(copy)
    def core_rows_of(k):
        at = cut(cell_of(k), share)

        def multiply(h, carry):
            here = cut(h, half)
            mine = part[cut(g, quarter), here]
            hi = mine.astype(bf16)
            rest = mine - hi.astype(f32)
            mid = rest.astype(bf16)
            low = (rest - mid.astype(f32)).astype(bf16)
            rows_left = left[at, cut(g, quarter)]
            core_part[at, here] = (
                jnp.dot(rows_left, hi, preferred_element_type=f32)
                + jnp.dot(rows_left, mid, preferred_element_type=f32)
                + jnp.dot(rows_left, low, preferred_element_type=f32)
            )
            return carry

        lax.fori_loop(0, 2, multiply, 0)

    own_share = cut(c, share)
    cc = []
    for k in range(1, n_cell):
        core_rows_of(k)
        copy = remote(
            core_part.at[cut(cell_of(k), share), :], core_cell.at[k - 1],
            cc_s.at[k - 1], cc_r.at[k - 1], cell=cell_of(k),
        )
        copy.start()
        cc.append(copy)
    core_rows_of(0)
    for k in range(1, n_cell):
        cc[k - 1].wait_recv()
        core_part[own_share, :] = core_part[own_share, :] + core_cell[k - 1]
    cg = []
    for i, peer in enumerate(gene_peers):
        src = pl.ds(pl.multiple_of(c * share + peer * core_rows, 8), core_rows)
        copy = remote(core_part.at[src, :], core_gene.at[i], cg_s.at[i], cg_r.at[i], gene=peer)
        copy.start()
        cg.append(copy)
    for j in range(lead, n_rank):
        left_piece(j, lambda copy: copy.start())

    for copy in agz[n_rank - 1 :]:
        copy.wait_recv()
    for copy in agx:
        copy.wait_recv()
    for j in range(lead):
        left_piece(j, lambda copy: copy.wait_recv())
    chunks = dense.shape[1] // GENE_CHUNK

    def gene_copy(k, j):
        return remote(
            gene_send.at[k - 1, :, cut(j, GENE_CHUNK)], gene_recv.at[k - 1, :, cut(j, GENE_CHUNK)],
            gs_s.at[k - 1, j], gs_r.at[k - 1, j], cell=cell_of(k),
        )

    for k in range(1, n_cell):
        peer_rows = cut(cell_of(k), share)

        def send_chunk(j, carry):
            gene_send[k - 1, :, cut(j, GENE_CHUNK)] = jnp.dot(
                left[peer_rows, :], dense[:, cut(j, GENE_CHUNK)], preferred_element_type=f32
            )
            gene_copy(k, j).start()
            return carry

        lax.fori_loop(0, chunks, send_chunk, 0)

    own_rows = pl.ds(pl.multiple_of(c * share + g * core_rows, 8), core_rows)
    for i in range(len(gene_peers)):
        cg[i].wait_recv()
        core_part[own_rows, :] = core_part[own_rows, :] + core_gene[i]
    cr = []
    for k in range(1, n_rank):
        copy = remote(
            core_part.at[own_rows, cut(rank_of(k), lanes)], core_rank.at[k - 1],
            cr_s.at[k - 1], cr_r.at[k - 1], rank=rank_of(k),
        )
        copy.start()
        cr.append(copy)

    final = core_part[own_rows, cut(r, lanes)]
    for k in range(1, n_rank):
        cr[k - 1].wait_recv()
        final = final + core_rank[k - 1]
    out_rows = pl.ds(pl.multiple_of(g * core_rows, 8), core_rows)
    core_out[out_rows, cut(r, lanes)] = final
    own_piece = core_out.at[out_rows, cut(r, lanes)]
    ar = []
    for k in range(1, n_rank):
        copy = remote(own_piece, own_piece, ar_s.at[k - 1], ar_r.at[k - 1], rank=rank_of(k))
        copy.start()
        ar.append(copy)
    rsz[-1].start()
    ag = []

    def spread(k):
        piece = core_out.at[out_rows, cut(rank_of(n_rank - k), lanes)]
        for i, peer in enumerate(gene_peers):
            copy = remote(piece, piece, ag_s.at[k, i], ag_r.at[k, i], gene=peer)
            copy.start()
            ag.append(copy)

    spread(0)
    for k in range(1, n_rank):
        ar[k - 1].wait_recv()
        spread(k)

    for j in range(lead, n_rank):
        left_piece(j, lambda copy: copy.wait_recv())

    def own_chunk(j, carry):
        here = cut(j, GENE_CHUNK)
        gene_out[:, here] = jnp.dot(left[own_share, :], dense[:, here], preferred_element_type=f32)
        return carry

    lax.fori_loop(0, chunks, own_chunk, 0)

    for k in range(1, n_cell):

        def add_chunk(j, carry):
            gene_copy(k, j).wait_recv()
            here = cut(j, GENE_CHUNK)
            gene_out[:, here] = gene_out[:, here] + gene_recv[k - 1, :, here]
            return carry

        lax.fori_loop(0, chunks, add_chunk, 0)

    for copy in rsz:
        copy.wait_recv()
    mine = part[pl.ds(pl.multiple_of(g * quarter + r * shard, shard), shard), :]
    for j in range(n_rank - 1):
        mine = mine + hopz[j]
    right_out[...] = mine
    for copy in ag:
        copy.wait_recv()

    for copy in agz + agx + [d0, d1, o0, o1] + second[0] + second[1] + rsz + cc + cg + cr + ar + ag:
        copy.wait_send()
    for j in range(n_rank):
        left_piece(j, lambda copy: copy.wait_send())
    for k in range(1, n_cell):

        def drain(j, carry):
            gene_copy(k, j).wait_send()
            return carry

        lax.fori_loop(0, chunks, drain, 0)


def body(sizes, blocks, block_pos, block_count, test_right, test_left, gene_sketch_old):
    n_cell, n_gene, n_rank = sizes
    f32, bf16 = jnp.float32, jnp.bfloat16
    tiles = blocks[0, 0]
    slots, brows, bcols = tiles.shape
    genes, width = test_right.shape
    rows, lw = test_left.shape
    left_width = lw * n_rank
    gene_blocks = genes // bcols
    places = (rows // brows) * gene_blocks
    slot_ids = jnp.arange(slots, dtype=jnp.int32)
    hit = (block_pos[0, 0][None, :] == jnp.arange(places, dtype=jnp.int32)[:, None]) & (
        slot_ids < block_count[0, 0]
    )[None, :]
    code = jnp.sum(jnp.where(hit, slot_ids[None, :] + 1, 0), axis=1).astype(jnp.int32)
    quarter, half = rows // n_gene, width // 2
    shard = quarter // n_rank
    share = left_width // n_cell
    core_rows, lanes = share // n_gene, width // n_rank
    chunks = genes // GENE_CHUNK
    dma = pltpu.SemaphoreType.DMA
    z, x = n_rank - 1, n_gene - 1

    def pair(*shape):
        return [dma(shape), dma(shape)]

    right_mine, gene_sum, core = pl.pallas_call(
        functools.partial(kernel, sizes),
        out_shape=(
            jax.ShapeDtypeStruct((shard, width), f32),
            jax.ShapeDtypeStruct((share, genes), f32),
            jax.ShapeDtypeStruct((share, width), f32),
        ),
        in_specs=[
            pl.BlockSpec(memory_space=pltpu.SMEM),
            pl.BlockSpec(memory_space=pltpu.HBM),
            pl.BlockSpec(memory_space=pltpu.HBM),
            pl.BlockSpec(memory_space=pltpu.HBM),
        ],
        out_specs=tuple(pl.BlockSpec(memory_space=pltpu.VMEM) for _ in range(3)),
        scratch_shapes=[
            pltpu.VMEM((slots, brows, bcols), bf16),
            pltpu.VMEM((rows, genes), bf16),
            pltpu.VMEM((genes, width), bf16),
            pltpu.VMEM((left_width, rows), bf16),
            pltpu.VMEM((rows, width), f32),
            pltpu.VMEM((4, quarter, half), f32),
            pltpu.VMEM((2, quarter, half), f32),
            pltpu.VMEM((z, shard, width), f32),
            pltpu.VMEM((left_width, width), f32),
            pltpu.VMEM((n_cell - 1, share, width), f32),
            pltpu.VMEM((x, core_rows, width), f32),
            pltpu.VMEM((z, core_rows, lanes), f32),
            pltpu.VMEM((n_cell - 1, share, genes), f32),
            pltpu.VMEM((n_cell - 1, share, genes), f32),
            dma((4,)),
            *pair(2 * z),
            *pair(n_rank + 1, 2),
            *pair(4),
            *pair(2 * n_rank),
            *pair(z),
            *pair(n_cell - 1),
            *pair(x),
            *pair(z),
            *pair(z),
            *pair(n_rank, x),
            *pair(n_cell - 1, chunks),
        ],
        compiler_params=pltpu.CompilerParams(
            collective_id=0, has_side_effects=True, vmem_limit_bytes=46 * 1024 * 1024
        ),
        name="sketch",
    )(code, tiles, test_right, test_left.T)
    return right_mine, gene_sketch_old + gene_sum, core


def solution(mesh):
    sizes = tuple(mesh.shape[name] for name in ("cell", "gene", "rank"))
    return jax.shard_map(
        functools.partial(body, sizes),
        mesh=mesh,
        in_specs=(
            P("cell", ("gene", "rank"), None, None, None),
            P("cell", ("gene", "rank"), None),
            P("cell", ("gene", "rank")),
            P(("gene", "rank"), None),
            P("cell", "rank"),
            P("cell", ("gene", "rank")),
        ),
        out_specs=(P(("cell", "gene", "rank"), None), P("cell", ("gene", "rank")), P("cell", None)),
        check_vma=False,
    )
```

```python
import functools

import jax
import jax.numpy as jnp
from jax import lax
from jax.experimental import pallas as pl
from jax.experimental.pallas import tpu as pltpu
from jax.sharding import PartitionSpec as P

MESH = pl.DeviceIdType.MESH
GENE_CHUNK = 256


def kernel(
    sizes, code, blocks, right_in, left_in, right_out, gene_out, core_out,
    tiles, dense, table, left, part, hop1, hop2, hopz,
    core_part, core_cell, core_gene, core_rank, gene_send, gene_recv,
    load_sem, agz_s, agz_r, agx_s, agx_r, rs1_s, rs1_r, rs2_s, rs2_r, rsz_s, rsz_r,
    cc_s, cc_r, cg_s, cg_r, cr_s, cr_r, ar_s, ar_r, ag_s, ag_r, gs_s, gs_r,
):
    n_cell, n_gene, n_rank = sizes
    f32, bf16 = jnp.float32, jnp.bfloat16
    c, g, r = lax.axis_index("cell"), lax.axis_index("gene"), lax.axis_index("rank")
    b1, b0 = g // 2, g % 2
    gx = 2 * b1 + (1 - b0)
    gy = 2 * (1 - b1) + b0
    gd = 2 * (1 - b1) + (1 - b0)
    gene_peers = [gx, gy, gd]
    rows, width = part.shape
    quarter = rows // n_gene
    shard = quarter // n_rank
    half = width // 2
    lw = left_in.shape[0]
    left_width = left.shape[0]
    brows, bcols = tiles.shape[1], tiles.shape[2]
    gene_blocks = dense.shape[1] // bcols
    share = left_width // n_cell
    core_rows = share // n_gene
    lanes = width // n_rank

    def rank_of(k):
        return lax.rem(r + k, n_rank)

    def cell_of(k):
        return lax.rem(c + k, n_cell)

    def cut(start, step):
        return pl.ds(pl.multiple_of(start * step, step), step)

    def remote(src, dst, ssem, rsem, **where):
        device = (where.get("cell", c), where.get("gene", g), where.get("rank", r))
        return pltpu.make_async_remote_copy(
            src_ref=src, dst_ref=dst, send_sem=ssem, recv_sem=rsem,
            device_id=device, device_id_type=MESH,
        )

    barrier = pltpu.get_barrier_semaphore()
    for k in range(1, n_rank):
        pl.semaphore_signal(barrier, inc=1, device_id=(c, g, rank_of(k)), device_id_type=MESH)
    for peer in gene_peers:
        pl.semaphore_signal(barrier, inc=1, device_id=(c, peer, r), device_id_type=MESH)
    for k in range(1, n_cell):
        pl.semaphore_signal(barrier, inc=1, device_id=(cell_of(k), g, r), device_id_type=MESH)

    load_tiles = pltpu.make_async_copy(blocks, tiles, load_sem.at[0])
    load_table = pltpu.make_async_copy(right_in, table, load_sem.at[1])
    load_tiles.start()
    load_table.start()
    own_left = pltpu.make_async_copy(left_in, left.at[cut(r, lw), :], load_sem.at[2])
    own_left.start()

    pl.semaphore_wait(barrier, (n_rank - 1) + len(gene_peers) + (n_cell - 1))

    agz = []
    for i, q in enumerate((g, gd)):
        for k in range(1, n_rank):
            s = i * (n_rank - 1) + k - 1
            copy = remote(
                left_in.at[:, cut(q, quarter)], left.at[cut(r, lw), cut(q, quarter)],
                agz_s.at[s], agz_r.at[s], rank=rank_of(k),
            )
            copy.start()
            agz.append(copy)
    load_tiles.wait()
    load_table.wait()

    row_blocks = quarter // brows

    def compute(q):
        def fill(i, carry):
            rb = q * row_blocks + i // gene_blocks
            gb = i % gene_blocks
            slot = code[rb * gene_blocks + gb]
            block = tiles[jnp.maximum(slot - 1, 0)]
            dense[cut(rb, brows), cut(gb, bcols)] = jnp.where(slot > 0, block, jnp.zeros_like(block))
            return carry

        lax.fori_loop(0, row_blocks * gene_blocks, fill, 0)

        def multiply(h, carry):
            part[cut(q, quarter), cut(h, half)] = jnp.dot(
                dense[cut(q, quarter), :], table[:, cut(h, half)], preferred_element_type=f32
            )
            return carry

        lax.fori_loop(0, 2, multiply, 0)

    h0, h1 = pl.ds(0, half), pl.ds(half, half)

    def rs1(i, q, h, peer):
        copy = remote(part.at[cut(q, quarter), h], hop1.at[i], rs1_s.at[i], rs1_r.at[i], gene=peer)
        copy.start()
        return copy

    compute(gd)
    d0 = rs1(0, gd, h0, gx)
    d1 = rs1(1, gd, h1, gy)
    compute(gx)
    o0 = rs1(2, gx, h0, gx)
    compute(gy)
    o1 = rs1(3, gy, h1, gy)
    compute(g)

    order = [rank_of(k) for k in range(1, n_rank)] + [r]
    second = []
    for i, (first, q, h, peer) in enumerate(((d0, gy, h0, gy), (d1, gx, h1, gx))):
        first.wait_recv()
        copies = []
        for j, z in enumerate(order):
            here = pl.ds(pl.multiple_of(q * quarter + z * shard, shard), shard)
            part[here, h] = part[here, h] + hop1[i, cut(z, shard), :]
            copy = remote(
                part.at[here, h], hop2.at[i, cut(z, shard), :],
                rs2_s.at[i * n_rank + j], rs2_r.at[i * n_rank + j], gene=peer,
            )
            copy.start()
            copies.append(copy)
        second.append(copies)

    own_left.wait()
    for copy in agz[: n_rank - 1]:
        copy.wait_recv()
    per_share = 0 if n_rank % n_cell else n_rank // n_cell
    lead = n_rank - per_share
    base = (c + 1) * per_share

    def left_piece(j, act):
        z = lax.rem(base + j, n_rank)
        here = left.at[cut(z, lw), cut(g, quarter)]

        @pl.when(z != r)
        def _():
            for i, peer in enumerate((gx, gy)):
                act(remote(here, here, agx_s.at[j, i], agx_r.at[j, i], gene=peer))

    for j in range(lead):
        left_piece(j, lambda copy: copy.start())

    o0.wait_recv()
    o1.wait_recv()
    rsz = []
    for j, z in enumerate(order):
        second[0][j].wait_recv()
        second[1][j].wait_recv()
        here = pl.ds(pl.multiple_of(g * quarter + z * shard, shard), shard)
        part[here, h0] = part[here, h0] + hop1[2, cut(z, shard), :] + hop2[0, cut(z, shard), :]
        part[here, h1] = part[here, h1] + hop1[3, cut(z, shard), :] + hop2[1, cut(z, shard), :]
        if j < n_rank - 1:
            copy = remote(part.at[here, :], hopz.at[j], rsz_s.at[j], rsz_r.at[j], rank=z)
            copy.start()
            rsz.append(copy)
    def core_rows_of(k):
        at = cut(cell_of(k), share)

        def multiply(h, carry):
            here = cut(h, half)
            mine = part[cut(g, quarter), here]
            hi = mine.astype(bf16)
            rest = mine - hi.astype(f32)
            mid = rest.astype(bf16)
            low = (rest - mid.astype(f32)).astype(bf16)
            rows_left = left[at, cut(g, quarter)]
            core_part[at, here] = (
                jnp.dot(rows_left, hi, preferred_element_type=f32)
                + jnp.dot(rows_left, mid, preferred_element_type=f32)
                + jnp.dot(rows_left, low, preferred_element_type=f32)
            )
            return carry

        lax.fori_loop(0, 2, multiply, 0)

    own_share = cut(c, share)
    cc = []
    for k in range(1, n_cell):
        core_rows_of(k)
        copy = remote(
            core_part.at[cut(cell_of(k), share), :], core_cell.at[k - 1],
            cc_s.at[k - 1], cc_r.at[k - 1], cell=cell_of(k),
        )
        copy.start()
        cc.append(copy)
    core_rows_of(0)
    for k in range(1, n_cell):
        cc[k - 1].wait_recv()
        core_part[own_share, :] = core_part[own_share, :] + core_cell[k - 1]
    cg = []
    for i, peer in enumerate(gene_peers):
        src = pl.ds(pl.multiple_of(c * share + peer * core_rows, 8), core_rows)
        copy = remote(core_part.at[src, :], core_gene.at[i], cg_s.at[i], cg_r.at[i], gene=peer)
        copy.start()
        cg.append(copy)
    for j in range(lead, n_rank):
        left_piece(j, lambda copy: copy.start())

    for copy in agz[n_rank - 1 :]:
        copy.wait_recv()
    for j in range(lead):
        left_piece(j, lambda copy: copy.wait_recv())
    chunks = dense.shape[1] // GENE_CHUNK

    def gene_copy(k, j):
        return remote(
            gene_send.at[k - 1, :, cut(j, GENE_CHUNK)], gene_recv.at[k - 1, :, cut(j, GENE_CHUNK)],
            gs_s.at[k - 1, j], gs_r.at[k - 1, j], cell=cell_of(k),
        )

    for k in range(1, n_cell):
        peer_rows = cut(cell_of(k), share)

        def send_chunk(j, carry):
            gene_send[k - 1, :, cut(j, GENE_CHUNK)] = jnp.dot(
                left[peer_rows, :], dense[:, cut(j, GENE_CHUNK)], preferred_element_type=f32
            )
            gene_copy(k, j).start()
            return carry

        lax.fori_loop(0, chunks, send_chunk, 0)

    own_rows = pl.ds(pl.multiple_of(c * share + g * core_rows, 8), core_rows)
    for i in range(len(gene_peers)):
        cg[i].wait_recv()
        core_part[own_rows, :] = core_part[own_rows, :] + core_gene[i]
    cr = []
    for k in range(1, n_rank):
        copy = remote(
            core_part.at[own_rows, cut(rank_of(k), lanes)], core_rank.at[k - 1],
            cr_s.at[k - 1], cr_r.at[k - 1], rank=rank_of(k),
        )
        copy.start()
        cr.append(copy)

    final = core_part[own_rows, cut(r, lanes)]
    for k in range(1, n_rank):
        cr[k - 1].wait_recv()
        final = final + core_rank[k - 1]
    out_rows = pl.ds(pl.multiple_of(g * core_rows, 8), core_rows)
    core_out[out_rows, cut(r, lanes)] = final
    own_piece = core_out.at[out_rows, cut(r, lanes)]
    ar = []
    for k in range(1, n_rank):
        copy = remote(own_piece, own_piece, ar_s.at[k - 1], ar_r.at[k - 1], rank=rank_of(k))
        copy.start()
        ar.append(copy)
    ag = []

    def spread(k):
        piece = core_out.at[out_rows, cut(rank_of(n_rank - k), lanes)]
        for i, peer in enumerate(gene_peers):
            copy = remote(piece, piece, ag_s.at[k, i], ag_r.at[k, i], gene=peer)
            copy.start()
            ag.append(copy)

    spread(0)
    for k in range(1, n_rank):
        ar[k - 1].wait_recv()
        spread(k)

    for j in range(lead, n_rank):
        left_piece(j, lambda copy: copy.wait_recv())

    def own_chunk(j, carry):
        here = cut(j, GENE_CHUNK)
        gene_out[:, here] = jnp.dot(left[own_share, :], dense[:, here], preferred_element_type=f32)
        return carry

    lax.fori_loop(0, chunks, own_chunk, 0)

    for k in range(1, n_cell):

        def add_chunk(j, carry):
            gene_copy(k, j).wait_recv()
            here = cut(j, GENE_CHUNK)
            gene_out[:, here] = gene_out[:, here] + gene_recv[k - 1, :, here]
            return carry

        lax.fori_loop(0, chunks, add_chunk, 0)

    for copy in rsz:
        copy.wait_recv()
    mine = part[pl.ds(pl.multiple_of(g * quarter + r * shard, shard), shard), :]
    for j in range(n_rank - 1):
        mine = mine + hopz[j]
    right_out[...] = mine
    for copy in ag:
        copy.wait_recv()

    for copy in agz + [d0, d1, o0, o1] + second[0] + second[1] + rsz + cc + cg + cr + ar + ag:
        copy.wait_send()
    for j in range(n_rank):
        left_piece(j, lambda copy: copy.wait_send())
    for k in range(1, n_cell):

        def drain(j, carry):
            gene_copy(k, j).wait_send()
            return carry

        lax.fori_loop(0, chunks, drain, 0)


def body(sizes, blocks, block_pos, block_count, test_right, test_left, gene_sketch_old):
    n_cell, n_gene, n_rank = sizes
    f32, bf16 = jnp.float32, jnp.bfloat16
    tiles = blocks[0, 0]
    slots, brows, bcols = tiles.shape
    genes, width = test_right.shape
    rows, lw = test_left.shape
    left_width = lw * n_rank
    gene_blocks = genes // bcols
    places = (rows // brows) * gene_blocks
    slot_ids = jnp.arange(slots, dtype=jnp.int32)
    hit = (block_pos[0, 0][None, :] == jnp.arange(places, dtype=jnp.int32)[:, None]) & (
        slot_ids < block_count[0, 0]
    )[None, :]
    code = jnp.sum(jnp.where(hit, slot_ids[None, :] + 1, 0), axis=1).astype(jnp.int32)
    quarter, half = rows // n_gene, width // 2
    shard = quarter // n_rank
    share = left_width // n_cell
    core_rows, lanes = share // n_gene, width // n_rank
    chunks = genes // GENE_CHUNK
    dma = pltpu.SemaphoreType.DMA
    z, x = n_rank - 1, n_gene - 1

    def pair(*shape):
        return [dma(shape), dma(shape)]

    right_mine, gene_sum, core = pl.pallas_call(
        functools.partial(kernel, sizes),
        out_shape=(
            jax.ShapeDtypeStruct((shard, width), f32),
            jax.ShapeDtypeStruct((share, genes), f32),
            jax.ShapeDtypeStruct((share, width), f32),
        ),
        in_specs=[
            pl.BlockSpec(memory_space=pltpu.SMEM),
            pl.BlockSpec(memory_space=pltpu.HBM),
            pl.BlockSpec(memory_space=pltpu.HBM),
            pl.BlockSpec(memory_space=pltpu.HBM),
        ],
        out_specs=tuple(pl.BlockSpec(memory_space=pltpu.VMEM) for _ in range(3)),
        scratch_shapes=[
            pltpu.VMEM((slots, brows, bcols), bf16),
            pltpu.VMEM((rows, genes), bf16),
            pltpu.VMEM((genes, width), bf16),
            pltpu.VMEM((left_width, rows), bf16),
            pltpu.VMEM((rows, width), f32),
            pltpu.VMEM((4, quarter, half), f32),
            pltpu.VMEM((2, quarter, half), f32),
            pltpu.VMEM((z, shard, width), f32),
            pltpu.VMEM((left_width, width), f32),
            pltpu.VMEM((n_cell - 1, share, width), f32),
            pltpu.VMEM((x, core_rows, width), f32),
            pltpu.VMEM((z, core_rows, lanes), f32),
            pltpu.VMEM((n_cell - 1, share, genes), f32),
            pltpu.VMEM((n_cell - 1, share, genes), f32),
            dma((3,)),
            *pair(2 * z),
            *pair(n_rank, 2),
            *pair(4),
            *pair(2 * n_rank),
            *pair(z),
            *pair(n_cell - 1),
            *pair(x),
            *pair(z),
            *pair(z),
            *pair(n_rank, x),
            *pair(n_cell - 1, chunks),
        ],
        compiler_params=pltpu.CompilerParams(
            collective_id=0, has_side_effects=True, vmem_limit_bytes=46 * 1024 * 1024
        ),
        name="sketch",
    )(code, tiles, test_right, test_left.T)
    return right_mine, gene_sketch_old + gene_sum, core


def solution(mesh):
    sizes = tuple(mesh.shape[name] for name in ("cell", "gene", "rank"))
    return jax.shard_map(
        functools.partial(body, sizes),
        mesh=mesh,
        in_specs=(
            P("cell", ("gene", "rank"), None, None, None),
            P("cell", ("gene", "rank"), None),
            P("cell", ("gene", "rank")),
            P(("gene", "rank"), None),
            P("cell", "rank"),
            P("cell", ("gene", "rank")),
        ),
        out_specs=(P(("cell", "gene", "rank"), None), P("cell", ("gene", "rank")), P("cell", None)),
        check_vma=False,
    )
```
